32 devices in a mesh: grp: 2 (over y), ep: 4 (over z), fs: 4 (over x, core).
Axes of the slice: x: 2, y: 2, z: 4, core: 2. Of those that a mesh axis runs over, the one named last changes fastest.
Arguments:
- tokens: bfloat16 [4096, 2048], P(('grp', 'ep', 'fs')), parts along dimension 0, may hold values from -6 to 6
- expert_ids: int32 [4096, 8], P(('grp', 'ep', 'fs')), parts along dimension 0, may hold values from 0 to 63, as said below
- gate_values: float32 [4096, 8], P(('grp', 'ep', 'fs')), parts along dimension 0, may hold values from 0.1 to 1
- w_gate: bfloat16 [64, 2048, 768], P('ep', None, 'fs'), may hold values from -0.125 to 0.125
- w_up: bfloat16 [64, 2048, 768], P('ep', None, 'fs'), may hold values from -0.125 to 0.125
- w_down: bfloat16 [64, 768, 2048], P('ep', 'fs'), may hold values from -0.21875 to 0.21875
Outputs:
- combined: bfloat16 [4096, 2048], P(('grp', 'ep', 'fs')), parts along dimension 0
The draws below stay inside these ranges and needn't reach their ends.
There are 2 independent parts, one for each index of `grp`. The reference program is written for one: setup_inputs(seed, part) draws one part's arguments, and reference() takes and returns one part's arrays. A program takes and returns all parts, laid end to end along the dimension named above; an argument that names none is the same for every part. Nothing has to cross between parts.
Inputs may be any that keep to these rules, and one draw needn't show every extreme that they name: `expert_ids`: each row names 8 different experts. In each aligned block of 128 rows (the rows of one device) no expert is named by more than 24 rows, and the 16 experts held by one index of ep, the same for all blocks, are each named by exactly 24 rows of every block.
All inputs are finite; a program needn't handle non-finite values.
Results may differ from the reference program's by a relative error of at most 0.0058.
Values may be sent and summed in bfloat16 or wider, within the bound.
A program may use at most 384 MiB of HBM per device.

```python
import math
import jax
import jax.numpy as jnp
from jax import lax

D = 2048
FF = 768
EXPERTS = 64
TOP = 8
TOK_DEV = 128
EXP_DEV = 16
TOKENS = 2048
ECAP = 24


def draw_expert_ids(key, part):
    blocks = TOKENS // TOK_DEV
    local_count = EXP_DEV
    groups = EXPERTS // EXP_DEV
    assigned = TOP * TOK_DEV
    remaining = assigned - local_count * ECAP
    others = EXPERTS - local_count
    base_load = remaining // others
    swing_size = max(min(base_load // 2, ECAP - base_load - 1), 0)
    extra_count = remaining - base_load * others
    hot_group = jax.random.randint(jax.random.fold_in(key, 11), (), 0, groups)
    labels = jnp.arange(EXPERTS, dtype=jnp.int32)
    is_hot = labels // local_count == hot_group

    def one_block(block_seed):
        subkeys = jax.random.split(block_seed, 4)
        score_one = jax.random.permutation(subkeys[0], EXPERTS).astype(jnp.int32)
        score_two = jax.random.permutation(subkeys[1], EXPERTS).astype(jnp.int32)
        rank_one = jnp.argsort(jnp.argsort(jnp.where(is_hot, EXPERTS + labels, score_one)))
        rank_two = jnp.argsort(jnp.argsort(jnp.where(is_hot, EXPERTS + labels, score_two)))
        counts = jnp.where(is_hot, ECAP, base_load + jnp.where(rank_one < others // 2, swing_size, -swing_size) + jnp.where(rank_two < extra_count, 1, 0)).astype(jnp.int32)
        run_order = jax.random.permutation(subkeys[2], EXPERTS).astype(jnp.int32)
        run_ends = jnp.cumsum(counts[run_order])
        positions = jnp.arange(assigned, dtype=jnp.int32)
        run_index = jnp.sum((run_ends[None, :] <= positions[:, None]).astype(jnp.int32), axis=1)
        listing = run_order[run_index]
        shuffle = jax.random.permutation(subkeys[3], TOK_DEV).astype(jnp.int32)
        where_at = jnp.arange(TOP, dtype=jnp.int32)[None, :] * TOK_DEV + shuffle[:, None]
        return listing[where_at]
    chosen = jax.vmap(one_block)(jax.random.split(jax.random.fold_in(key, 23), blocks))
    return chosen.reshape(TOKENS, TOP).astype(jnp.int32)


def block_scale(stream_key, shape, pieces, smallest, top_value):
    def one(axis_at, parts):
        draws = jax.random.uniform(jax.random.fold_in(jax.random.fold_in(stream_key, 6), axis_at), (parts,), jnp.float32, smallest / len(pieces), top_value / len(pieces))
        return jnp.repeat(jnp.exp(draws), shape[axis_at] // parts).reshape((-1,) + (1,) * (len(shape) - axis_at - 1))

    factor_of = one(*pieces[0])
    for cut in pieces[1:]:
        factor_of = factor_of * one(*cut)
    return factor_of


def bell_draw(rng, extent, scale, limit, cuts=(), kind=jnp.bfloat16):
    result = jax.random.normal(rng, extent, jnp.float32) * scale
    if len(cuts) > 0:
        result = block_scale(rng, extent, cuts, -0.22, 0.18) * result
    return jnp.clip(result, min=-limit, max=limit).astype(kind)


def setup_inputs(seed: int = 0, part: int = 0) -> dict:
    key_list = jax.random.split(jax.random.key(seed), 7)
    part_splits = jax.random.split(jax.random.fold_in(key_list[6], part), 7)
    tokens = bell_draw(part_splits[0], (TOKENS, D), 1.0, 6.0, ((0, 16),))
    expert_ids = draw_expert_ids(jax.random.fold_in(jax.random.fold_in(key_list[6], part), 71), part)
    gate_values = jnp.clip(jnp.exp(math.log(1.0) - 2.3025851 * jax.random.uniform(part_splits[2], (TOKENS, TOP), jnp.float32) ** block_scale(part_splits[2], (TOKENS, TOP), ((0, 16),), -0.2, 0.2)), 0.1, 1.0)
    w_gate = bell_draw(key_list[3], (EXPERTS, D, FF), D ** -0.5, 0.125, ((0, 4), (2, 4)))
    w_up = bell_draw(key_list[4], (EXPERTS, D, FF), D ** -0.5, 0.125, ((0, 4), (2, 4)))
    w_down = bell_draw(key_list[5], (EXPERTS, FF, D), FF ** -0.5, 0.21875, ((0, 4), (1, 4)))
    return dict(tokens=tokens, expert_ids=expert_ids, gate_values=gate_values, w_gate=w_gate, w_up=w_up, w_down=w_down)


def reference(tokens, expert_ids, gate_values, w_gate, w_up, w_down):
    flat_ids = expert_ids.reshape(-1)
    flat_gates = gate_values.reshape(-1)
    capacity = ECAP * (TOKENS // TOK_DEV)

    def one_expert(running, expert):
        selected = flat_ids == expert
        live_count = jnp.sum(selected.astype(jnp.int32))
        pair_index = jnp.nonzero(selected, size=capacity, fill_value=0)[0].astype(jnp.int32)
        live_rows = jnp.arange(capacity, dtype=jnp.int32) < live_count
        token_rows = pair_index // TOP
        chosen = tokens[token_rows]
        gate_pre = jnp.dot(chosen, w_gate[expert], preferred_element_type=jnp.float32)
        up_pre = jnp.dot(chosen, w_up[expert], preferred_element_type=jnp.float32)
        hidden = (jax.nn.silu(gate_pre) * up_pre).astype(jnp.bfloat16)
        expert_out = jnp.dot(hidden, w_down[expert], preferred_element_type=jnp.float32).astype(jnp.bfloat16)
        weighted = jnp.where(live_rows[:, None], flat_gates[pair_index][:, None] * expert_out.astype(jnp.float32), 0.0)
        return running.at[token_rows].add(weighted), None

    running, _ = lax.scan(one_expert, jnp.zeros((TOKENS, D), jnp.float32), jnp.arange(EXPERTS, dtype=jnp.int32))
    return running.astype(jnp.bfloat16)
```

```python
import jax
import jax.numpy as jnp
from jax import lax
from jax.sharding import PartitionSpec as P

ECAP = 24


def on_device(tokens, expert_ids, gate_values, w_gate, w_up, w_down):
    row_count, model_width = tokens.shape
    top_count = expert_ids.shape[1]
    local_count = w_gate.shape[0]
    axes = ("ep", "fs")
    blocks = lax.axis_size("ep") * lax.axis_size("fs")
    packed = jnp.concatenate([expert_ids.astype(jnp.float32), gate_values], axis=1)
    all_tokens = lax.all_gather(tokens, axes, axis=0, tiled=False)
    all_packed = lax.all_gather(packed, axes, axis=0, tiled=False)
    ids = all_packed[:, :, :top_count].astype(jnp.int32)
    gates = all_packed[:, :, top_count:]
    mine = lax.axis_index("ep") * local_count + jnp.arange(local_count, dtype=jnp.int32)
    match = ids[:, :, :, None] == mine
    member = jnp.any(match, axis=2)
    weight = jnp.sum(jnp.where(match, gates[:, :, :, None], 0.0), axis=2)
    place = jnp.cumsum(member.astype(jnp.int32), axis=1) - 1
    place = jnp.where(member, place, -1)
    pick = place.transpose(0, 2, 1)[:, :, None, :] == jnp.arange(ECAP, dtype=jnp.int32)[:, None]
    slot_weight = jnp.sum(
        jnp.where(pick, weight.transpose(0, 2, 1)[:, :, None, :], 0.0), axis=3
    )
    pick = pick.astype(jnp.bfloat16)
    rows = jnp.einsum("best,btd->besd", pick, all_tokens)
    rows = rows.transpose(1, 0, 2, 3).reshape(local_count, blocks * ECAP, model_width)
    gate_part = jnp.einsum("erd,edf->erf", rows, w_gate, preferred_element_type=jnp.float32)
    up_part = jnp.einsum("erd,edf->erf", rows, w_up, preferred_element_type=jnp.float32)
    hidden = (jax.nn.silu(gate_part) * up_part).astype(jnp.bfloat16)
    results = jnp.einsum("erf,efd->erd", hidden, w_down, preferred_element_type=jnp.float32)
    results = results.reshape(local_count, blocks, ECAP, model_width)
    results = (results * slot_weight.transpose(1, 0, 2)[:, :, :, None]).astype(jnp.bfloat16)
    partial = jnp.einsum(
        "best,ebsd->btd", pick, results, preferred_element_type=jnp.float32
    ).astype(jnp.bfloat16)
    summed = lax.psum_scatter(
        partial.reshape(blocks * row_count, model_width), axes, scatter_dimension=0, tiled=True
    )
    return summed


def solution(mesh):
    placed = (
        P(("grp", "ep", "fs"), None),
        P(("grp", "ep", "fs"), None),
        P(("grp", "ep", "fs"), None),
        P("ep", None, "fs"),
        P("ep", None, "fs"),
        P("ep", "fs", None),
    )
    return jax.shard_map(
        on_device,
        mesh=mesh,
        in_specs=placed,
        out_specs=P(("grp", "ep", "fs"), None),
        check_vma=False,
    )
```

```python
import functools

import jax
import jax.numpy as jnp
from jax import lax
from jax.experimental import pallas as pl
from jax.experimental.pallas import tpu as pltpu
from jax.sharding import PartitionSpec as P

ECAP = 24
CHUNK = 512
WBUF = 3
MESH = pl.DeviceIdType.MESH


def fused_kernel(
    tok_ref, meta_in, wg_hbm, wu_hbm, wd_hbm, out_ref,
    hold, meta, rows, slotw, pick, pickt, wbuf, core_buf, x_buf, z_buf,
    own_sem, w_sem, m_send, m_recv, z_send, z_recv, x_send, x_recv, c_send, c_recv,
    r1_send, r1_recv, r2_send, r2_recv, r3_send, r3_recv,
):
    experts = wg_hbm.shape[0]
    ff = wg_hbm.shape[1]
    width = tok_ref.shape[1]
    tok = tok_ref.shape[0]
    pair_slots = 2 * ECAP
    top = meta_in.shape[0] // 2
    e_me = lax.axis_index("ep")
    f_me = lax.axis_index("fs")
    x_me = f_me // 2
    c_me = lax.rem(f_me, 2)
    b_me = e_me * 4 + f_me
    f_xn = (1 - x_me) * 2 + c_me
    f_cn = x_me * 2 + 1 - c_me

    def remote(source, target, ssem, rsem, ep, fs):
        return pltpu.make_async_remote_copy(
            src_ref=source, dst_ref=target, send_sem=ssem, recv_sem=rsem,
            device_id={"ep": ep, "fs": fs}, device_id_type=MESH,
        )

    def weight_copies(e, slot):
        return [
            pltpu.make_async_copy(w.at[e], wbuf.at[slot, i], w_sem.at[slot, i])
            for i, w in enumerate((wg_hbm, wu_hbm, wd_hbm))
        ]

    own = pltpu.make_async_copy(tok_ref, hold.at[b_me], own_sem.at[0])
    own_meta = pltpu.make_async_copy(meta_in, meta.at[b_me], own_sem.at[1])
    own.start()
    own_meta.start()
    for e in range(WBUF):
        for copy in weight_copies(e, e):
            copy.start()

    barrier = pltpu.get_barrier_semaphore()
    for i in range(1, 16):
        peer = lax.rem(b_me + i, 16)
        pl.semaphore_signal(
            barrier, inc=1, device_id={"ep": peer // 4, "fs": lax.rem(peer, 4)},
            device_id_type=MESH,
        )
    pl.semaphore_wait(barrier, 15)

    def z_copy(k):
        return remote(
            tok_ref, hold.at[b_me], z_send.at[k - 1], z_recv.at[k - 1],
            lax.rem(e_me + k, 4), f_me,
        )

    def group(j):
        return lax.rem(e_me + 4 - j, 4)

    def x_copy(j):
        block = hold.at[group(j) * 4 + f_me]
        return remote(block, block, x_send.at[j], x_recv.at[j], e_me, f_xn)

    def c_copy(j, other):
        block = hold.at[group(j) * 4 + (f_xn if other else f_me)]
        return remote(
            block, block, c_send.at[j * 2 + other], c_recv.at[j * 2 + other], e_me, f_cn
        )

    def meta_copy(i):
        peer = lax.rem(b_me + i, 16)
        return remote(
            meta_in, meta.at[b_me], m_send.at[i - 1], m_recv.at[i - 1],
            peer // 4, lax.rem(peer, 4),
        )

    for i in range(1, 16):
        meta_copy(i).start()
    for k in (1, 2, 3):
        z_copy(k).start()
    own.wait()
    own_meta.wait()
    x_copy(0).start()
    c_copy(0, 0).start()
    for i in range(1, 16):
        source = lax.rem(b_me + 16 - i, 16)
        remote(
            meta_in, meta.at[source], m_send.at[i - 1], m_recv.at[i - 1],
            source // 4, lax.rem(source, 4),
        ).wait_recv()

    def dispatch(q, first):
        ids_row = lax.broadcasted_iota(jnp.int32, (experts, tok), 0)
        wanted = (ids_row + e_me * experts).astype(jnp.float32)
        upper = (
            lax.broadcasted_iota(jnp.int32, (tok, tok), 0)
            <= lax.broadcasted_iota(jnp.int32, (tok, tok), 1)
        ).astype(jnp.float32).astype(jnp.bfloat16)
        places, weights = [], []
        for half in range(2):
            table = meta[first + half]
            member = jnp.zeros((experts, tok), jnp.float32)
            weight = jnp.zeros((experts, tok), jnp.float32)
            for k in range(top):
                same = table[k : k + 1, :] == wanted
                member = jnp.where(same, 1.0, member)
                weight = jnp.where(same, table[top + k : top + k + 1, :], weight)
            count = jnp.dot(
                member.astype(jnp.bfloat16), upper, preferred_element_type=jnp.float32
            )
            places.append(jnp.where(member > 0.5, count - 1.0 + half * ECAP, -1.0))
            weights.append(weight)
        place = jnp.concatenate(places, axis=1)
        weight = jnp.concatenate(weights, axis=1)
        slot = lax.broadcasted_iota(jnp.int32, (pair_slots, 2 * tok), 0).astype(jnp.float32)
        base = pl.multiple_of(q * pair_slots, pair_slots)
        for e in range(experts):
            hit = place[e : e + 1, :] == slot
            pick[e * pair_slots : (e + 1) * pair_slots, :] = jnp.where(hit, 1.0, 0.0)
            value = jnp.sum(
                jnp.where(hit, weight[e : e + 1, :], 0.0), axis=1, keepdims=True
            )
            slotw[e, pl.ds(base, pair_slots), :] = jnp.broadcast_to(value, (pair_slots, 128))
        pickt[q] = jnp.transpose(pick[...]).astype(jnp.bfloat16)

        def part(n, carry):
            columns = pl.ds(pl.multiple_of(n * CHUNK, CHUNK), CHUNK)
            block = hold[pl.ds(first, 2), :, columns].reshape(2 * tok, CHUNK)
            got = jnp.dot(
                pick[...].astype(jnp.bfloat16), block, preferred_element_type=jnp.float32
            )
            rows[:, pl.ds(base, pair_slots), columns] = got.astype(jnp.bfloat16).reshape(
                experts, pair_slots, CHUNK
            )
            return carry

        lax.fori_loop(0, width // CHUNK, part, 0)

    def c_arrival(j, other):
        f_from = (1 - x_me if other else x_me) * 2 + 1 - c_me
        block = hold.at[group(j) * 4 + f_from]
        return remote(
            block, block, c_send.at[j * 2 + other], c_recv.at[j * 2 + other], e_me, f_cn
        )

    def gather_step(j, carry):
        @pl.when(j > 0)
        def _():
            block = hold.at[group(j) * 4 + f_me]
            remote(
                tok_ref, block, z_send.at[j - 1], z_recv.at[j - 1], group(j), f_me
            ).wait_recv()
            x_copy(j).start()
            c_copy(j, 0).start()

        c_arrival(j, 0).wait_recv()
        dispatch(2 * j, group(j) * 4 + x_me * 2)
        block = hold.at[group(j) * 4 + f_xn]
        remote(block, block, x_send.at[j], x_recv.at[j], e_me, f_xn).wait_recv()
        c_copy(j, 1).start()
        c_arrival(j, 1).wait_recv()
        dispatch(2 * j + 1, group(j) * 4 + (1 - x_me) * 2)
        return carry

    lax.fori_loop(0, 4, gather_step, 0)
    for i in range(1, 16):
        meta_copy(i).wait_send()
    for k in (1, 2, 3):
        z_copy(k).wait_send()
    for j in range(4):
        x_copy(j).wait_send()
        c_copy(j, 0).wait_send()
        c_copy(j, 1).wait_send()

    def expert_step(e, carry):
        slot = lax.rem(e, WBUF)
        for copy in weight_copies(e, slot):
            copy.wait()
        given = rows[e]
        over = (((1,), (1,)), ((), ()))
        gate = lax.dot_general(
            given, wbuf[slot, 0], over, preferred_element_type=jnp.float32
        )
        up = lax.dot_general(given, wbuf[slot, 1], over, preferred_element_type=jnp.float32)
        hidden = (gate / (1.0 + jnp.exp(-gate)) * up).astype(jnp.bfloat16)
        scale = jnp.concatenate([slotw[e]] * (CHUNK // 128), axis=1)
        for n in range(width // CHUNK):
            columns = slice(n * CHUNK, (n + 1) * CHUNK)
            result = jnp.dot(
                hidden, wbuf[slot, 2, :, columns], preferred_element_type=jnp.float32
            )
            rows[e, :, columns] = (result * scale).astype(jnp.bfloat16)

        @pl.when(e + WBUF < experts)
        def _():
            for copy in weight_copies(e + WBUF, slot):
                copy.start()

        return carry

    lax.fori_loop(0, experts, expert_step, 0)

    def combine(q):
        base = pl.multiple_of(q * pair_slots, pair_slots)

        def part(n, carry):
            columns = pl.ds(pl.multiple_of(n * CHUNK, CHUNK), CHUNK)
            block = rows[:, pl.ds(base, pair_slots), columns].reshape(
                experts * pair_slots, CHUNK
            )
            got = jnp.dot(pickt[q], block, preferred_element_type=jnp.float32)
            got = got.astype(jnp.bfloat16)
            hold[2 * q + c_me, :, columns] = got[:tok]
            hold[2 * q + 1 - c_me, :, columns] = got[tok:]
            return carry

        lax.fori_loop(0, width // CHUNK, part, 0)

    def r1_copy(q):
        return remote(
            hold.at[2 * q + 1], core_buf.at[q], r1_send.at[q], r1_recv.at[q], e_me, f_cn
        )

    def r2_copy(j):
        return remote(
            hold.at[4 * j + 2], x_buf.at[j], r2_send.at[j], r2_recv.at[j], e_me, f_xn
        )

    def r3_copy(j):
        return remote(
            hold.at[4 * j], z_buf.at[j - 1], r3_send.at[j - 1], r3_recv.at[j - 1],
            group(j), f_me,
        )

    def finish(j):
        r1_copy(2 * j).wait_recv()
        r2_copy(j).wait_recv()
        return (
            hold[4 * j].astype(jnp.float32)
            + core_buf[2 * j].astype(jnp.float32)
            + x_buf[j].astype(jnp.float32)
        )

    def scatter_step(s, carry):
        j = lax.rem(s + 1, 4)
        combine(2 * j + 1)
        r1_copy(2 * j + 1).start()
        combine(2 * j)
        r1_copy(2 * j).start()
        r1_copy(2 * j + 1).wait_recv()
        hold[4 * j + 2] = (
            hold[4 * j + 2].astype(jnp.float32) + core_buf[2 * j + 1].astype(jnp.float32)
        ).astype(jnp.bfloat16)
        r2_copy(j).start()

        @pl.when(s > 0)
        def _():
            hold[4 * s] = finish(s).astype(jnp.bfloat16)
            r3_copy(s).start()

        return carry

    lax.fori_loop(0, 4, scatter_step, 0)
    total = finish(0)
    for j in (1, 2, 3):
        r3_copy(j).wait_recv()
        total = total + z_buf[j - 1].astype(jnp.float32)
    out_ref[...] = total.astype(jnp.bfloat16)
    for q in range(8):
        r1_copy(q).wait_send()
    for j in range(4):
        r2_copy(j).wait_send()
    for j in (1, 2, 3):
        r3_copy(j).wait_send()


def on_device_fused(tokens, expert_ids, gate_values, w_gate, w_up, w_down):
    tok, width = tokens.shape
    experts, ff = w_down.shape[:2]
    packed = jnp.concatenate([expert_ids.T.astype(jnp.float32), gate_values.T], axis=0)
    bf16, f32 = jnp.bfloat16, jnp.float32
    dma = pltpu.SemaphoreType.DMA
    vmem = pl.BlockSpec(memory_space=pltpu.VMEM)
    hbm = pl.BlockSpec(memory_space=pl.ANY)
    slots = 16 * ECAP
    return pl.pallas_call(
        fused_kernel,
        out_shape=jax.ShapeDtypeStruct((tok, width), bf16),
        in_specs=[vmem, vmem, hbm, hbm, hbm],
        out_specs=vmem,
        scratch_shapes=[
            pltpu.VMEM((16, tok, width), bf16),
            pltpu.VMEM((16,) + packed.shape, f32),
            pltpu.VMEM((experts, slots, width), bf16),
            pltpu.VMEM((experts, slots, 128), f32),
            pltpu.VMEM((experts * 2 * ECAP, 2 * tok), f32),
            pltpu.VMEM((8, 2 * tok, experts * 2 * ECAP), bf16),
            pltpu.VMEM((WBUF, 3, ff, width), bf16),
            pltpu.VMEM((8, tok, width), bf16),
            pltpu.VMEM((4, tok, width), bf16),
            pltpu.VMEM((3, tok, width), bf16),
            dma((2,)), dma((WBUF, 3)), dma((15,)), dma((15,)),
            dma((3,)), dma((3,)), dma((4,)), dma((4,)), dma((8,)), dma((8,)),
            dma((8,)), dma((8,)), dma((4,)), dma((4,)), dma((3,)), dma((3,)),
        ],
        compiler_params=pltpu.CompilerParams(
            collective_id=0, has_side_effects=True, vmem_limit_bytes=63 * 1024 * 1024
        ),
    )(tokens, packed, w_gate.swapaxes(1, 2), w_up.swapaxes(1, 2), w_down)


def on_device(tokens, expert_ids, gate_values, w_gate, w_up, w_down):
    row_count, model_width = tokens.shape
    top_count = expert_ids.shape[1]
    local_count = w_gate.shape[0]
    axes = ("ep", "fs")
    blocks = lax.axis_size("ep") * lax.axis_size("fs")
    packed = jnp.concatenate([expert_ids.astype(jnp.float32), gate_values], axis=1)
    all_tokens = lax.all_gather(tokens, axes, axis=0, tiled=False)
    all_packed = lax.all_gather(packed, axes, axis=0, tiled=False)
    ids = all_packed[:, :, :top_count].astype(jnp.int32)
    gates = all_packed[:, :, top_count:]
    mine = lax.axis_index("ep") * local_count + jnp.arange(local_count, dtype=jnp.int32)
    match = ids[:, :, :, None] == mine
    member = jnp.any(match, axis=2)
    weight = jnp.sum(jnp.where(match, gates[:, :, :, None], 0.0), axis=2)
    place = jnp.cumsum(member.astype(jnp.int32), axis=1) - 1
    place = jnp.where(member, place, -1)
    pick = place.transpose(0, 2, 1)[:, :, None, :] == jnp.arange(ECAP, dtype=jnp.int32)[:, None]
    slot_weight = jnp.sum(
        jnp.where(pick, weight.transpose(0, 2, 1)[:, :, None, :], 0.0), axis=3
    )
    pick = pick.astype(jnp.bfloat16)
    rows = jnp.einsum("best,btd->besd", pick, all_tokens)
    rows = rows.transpose(1, 0, 2, 3).reshape(local_count, blocks * ECAP, model_width)
    gate_part = jnp.einsum("erd,edf->erf", rows, w_gate, preferred_element_type=jnp.float32)
    up_part = jnp.einsum("erd,edf->erf", rows, w_up, preferred_element_type=jnp.float32)
    hidden = (jax.nn.silu(gate_part) * up_part).astype(jnp.bfloat16)
    results = jnp.einsum("erf,efd->erd", hidden, w_down, preferred_element_type=jnp.float32)
    results = results.reshape(local_count, blocks, ECAP, model_width)
    results = (results * slot_weight.transpose(1, 0, 2)[:, :, :, None]).astype(jnp.bfloat16)
    partial = jnp.einsum(
        "best,ebsd->btd", pick, results, preferred_element_type=jnp.float32
    ).astype(jnp.bfloat16)
    summed = lax.psum_scatter(
        partial.reshape(blocks * row_count, model_width), axes, scatter_dimension=0, tiled=True
    )
    return summed


def solution(mesh):
    placed = (
        P(("grp", "ep", "fs"), None),
        P(("grp", "ep", "fs"), None),
        P(("grp", "ep", "fs"), None),
        P("ep", None, "fs"),
        P("ep", None, "fs"),
        P("ep", "fs", None),
    )
    small = mesh.shape["ep"] == 4 and mesh.shape["fs"] == 4
    return jax.shard_map(
        on_device_fused if small else on_device,
        mesh=mesh,
        in_specs=placed,
        out_specs=P(("grp", "ep", "fs"), None),
        check_vma=False,
    )
```

```python
import jax
import jax.numpy as jnp
from jax import lax
from jax.experimental import pallas as pl
from jax.experimental.pallas import tpu as pltpu
from jax.sharding import PartitionSpec as P

ECAP = 24
CHUNK = 512
WBUF = 3
MESH = pl.DeviceIdType.MESH


def fused_kernel(
    tok_ref, meta_in, wg_hbm, wu_hbm, wd_hbm, out_ref,
    hold, meta, rows, slotw, pick, pickt, wbuf, core_buf, x_buf, z_buf, done,
    own_sem, w_sem, m_send, m_recv, up_send, down_send, z_recv, x_send, x_recv, c_send, c_recv,
    r1_send, r1_recv, r2_send, r2_recv, r3_send, r3_recv,
):
    experts = wg_hbm.shape[0]
    width = tok_ref.shape[1]
    tok = tok_ref.shape[0]
    pair_slots = 2 * ECAP
    top = meta_in.shape[0] // 2
    e_me = lax.axis_index("ep")
    f_me = lax.axis_index("fs")
    x_me = f_me // 2
    c_me = lax.rem(f_me, 2)
    b_me = e_me * 4 + f_me
    f_xn = (1 - x_me) * 2 + c_me
    f_cn = x_me * 2 + 1 - c_me

    def remote(source, target, ssem, rsem, ep, fs):
        return pltpu.make_async_remote_copy(
            src_ref=source, dst_ref=target, send_sem=ssem, recv_sem=rsem,
            device_id={"ep": ep, "fs": fs}, device_id_type=MESH,
        )

    def weight_copies(e, slot):
        return [
            pltpu.make_async_copy(w.at[e], wbuf.at[slot, i], w_sem.at[slot, i])
            for i, w in enumerate((wg_hbm, wu_hbm, wd_hbm))
        ]

    own = pltpu.make_async_copy(tok_ref, hold.at[b_me], own_sem.at[0])
    own_meta = pltpu.make_async_copy(meta_in, meta.at[b_me], own_sem.at[1])
    own.start()
    own_meta.start()
    for e in range(WBUF):
        for copy in weight_copies(e, e):
            copy.start()

    barrier = pltpu.get_barrier_semaphore()
    for i in range(1, 16):
        peer = lax.rem(b_me + i, 16)
        pl.semaphore_signal(
            barrier, inc=1, device_id={"ep": peer // 4, "fs": lax.rem(peer, 4)},
            device_id_type=MESH,
        )
    pl.semaphore_wait(barrier, 15)

    def group(j):
        if isinstance(j, int) and j == 0:
            return e_me
        if j == 1:
            return jnp.where(e_me == 0, 1, e_me - 1)
        if j == 2:
            return jnp.where(e_me == 0, 2, jnp.where(e_me == 3, 1, e_me + 1))
        return jnp.where(e_me < 2, 3, 0)

    def z_copy(ep, up):
        block = hold.at[ep * 4 + f_me]
        sems = up_send if up else down_send
        return remote(
            block, block, sems.at[ep], z_recv.at[ep], e_me + 1 if up else e_me - 1, f_me
        )

    def z_arrival(ep):
        block = hold.at[ep * 4 + f_me]
        return remote(block, block, up_send.at[ep], z_recv.at[ep], lax.rem(e_me + 1, 4), f_me)

    def x_copy(j):
        block = hold.at[group(j) * 4 + f_me]
        return remote(block, block, x_send.at[j], x_recv.at[j], e_me, f_xn)

    def c_copy(j, other):
        block = hold.at[group(j) * 4 + (f_xn if other else f_me)]
        return remote(
            block, block, c_send.at[j * 2 + other], c_recv.at[j * 2 + other], e_me, f_cn
        )

    def meta_copy(i):
        peer = lax.rem(b_me + i, 16)
        return remote(
            meta_in, meta.at[b_me], m_send.at[i - 1], m_recv.at[i - 1],
            peer // 4, lax.rem(peer, 4),
        )

    for i in range(1, 16):
        meta_copy(i).start()
    own.wait()
    own_meta.wait()

    def relay(ep, act):
        @pl.when(jnp.logical_and(ep <= e_me, e_me < 3))
        def _():
            act(z_copy(ep, True))

        @pl.when(jnp.logical_and(ep >= e_me, e_me > 0))
        def _():
            act(z_copy(ep, False))

    relay(e_me, lambda copy: copy.start())
    x_copy(0).start()
    c_copy(0, 0).start()
    for i in range(1, 16):
        source = lax.rem(b_me + 16 - i, 16)
        remote(
            meta_in, meta.at[source], m_send.at[i - 1], m_recv.at[i - 1],
            source // 4, lax.rem(source, 4),
        ).wait_recv()

    def dispatch(q, first):
        ids_row = lax.broadcasted_iota(jnp.int32, (experts, tok), 0)
        wanted = (ids_row + e_me * experts).astype(jnp.float32)
        upper = (
            lax.broadcasted_iota(jnp.int32, (tok, tok), 0)
            <= lax.broadcasted_iota(jnp.int32, (tok, tok), 1)
        ).astype(jnp.float32).astype(jnp.bfloat16)
        places, weights = [], []
        for half in range(2):
            table = meta[first + half]
            member = jnp.zeros((experts, tok), jnp.float32)
            weight = jnp.zeros((experts, tok), jnp.float32)
            for k in range(top):
                same = table[k : k + 1, :] == wanted
                member = jnp.where(same, 1.0, member)
                weight = jnp.where(same, table[top + k : top + k + 1, :], weight)
            count = jnp.dot(
                member.astype(jnp.bfloat16), upper, preferred_element_type=jnp.float32
            )
            places.append(jnp.where(member > 0.5, count - 1.0 + half * ECAP, -1.0))
            weights.append(weight)
        place = jnp.concatenate(places, axis=1)
        weight = jnp.concatenate(weights, axis=1)
        slot = lax.broadcasted_iota(jnp.int32, (pair_slots, 2 * tok), 0).astype(jnp.float32)
        base = pl.multiple_of(q * pair_slots, pair_slots)
        for e in range(experts):
            hit = place[e : e + 1, :] == slot
            pick[e * pair_slots : (e + 1) * pair_slots, :] = jnp.where(hit, 1.0, 0.0)
            value = jnp.sum(
                jnp.where(hit, weight[e : e + 1, :], 0.0), axis=1, keepdims=True
            )
            slotw[e, pl.ds(q % 4 * pair_slots, pair_slots), :] = jnp.broadcast_to(value, (pair_slots, 128))
        pickt[q] = jnp.transpose(pick[...]).astype(jnp.bfloat16)

        def part(n, carry):
            columns = pl.ds(pl.multiple_of(n * CHUNK, CHUNK), CHUNK)
            block = hold[pl.ds(first, 2), :, columns].reshape(2 * tok, CHUNK)
            got = jnp.dot(
                pick[...].astype(jnp.bfloat16), block, preferred_element_type=jnp.float32
            )
            rows[:, pl.ds(base, pair_slots), columns] = got.astype(jnp.bfloat16).reshape(
                experts, pair_slots, CHUNK
            )
            return carry

        lax.fori_loop(0, width // CHUNK, part, 0)

    def c_arrival(j, other):
        f_from = (1 - x_me if other else x_me) * 2 + 1 - c_me
        block = hold.at[group(j) * 4 + f_from]
        return remote(
            block, block, c_send.at[j * 2 + other], c_recv.at[j * 2 + other], e_me, f_cn
        )

    def pass_on(j):
        if j > 0:
            ep = group(j)
            z_arrival(ep).wait_recv()
            relay(ep, lambda copy: copy.start())
            x_copy(j).start()
            c_copy(j, 0).start()

    def pass_across(j):
        block = hold.at[group(j) * 4 + f_xn]
        remote(block, block, x_send.at[j], x_recv.at[j], e_me, f_xn).wait_recv()
        c_copy(j, 1).start()

    def take(j, other):
        c_arrival(j, other).wait_recv()
        f_base = (1 - x_me if other else x_me) * 2
        dispatch(2 * j + other, group(j) * 4 + f_base)

    half_rows = 4 * pair_slots

    def expert_step(t, half):
        e = lax.rem(t, experts)
        slot = lax.rem(t, WBUF)
        for copy in weight_copies(e, slot):
            copy.wait()
        part = slice(half * half_rows, (half + 1) * half_rows)
        given = rows[e, part, :]
        over = (((1,), (1,)), ((), ()))
        gate = lax.dot_general(
            given, wbuf[slot, 0], over, preferred_element_type=jnp.float32
        )
        up = lax.dot_general(given, wbuf[slot, 1], over, preferred_element_type=jnp.float32)
        hidden = (gate / (1.0 + jnp.exp(-gate)) * up).astype(jnp.bfloat16)
        scale = jnp.concatenate([slotw[e]] * (CHUNK // 128), axis=1)
        for n in range(width // CHUNK):
            columns = slice(n * CHUNK, (n + 1) * CHUNK)
            result = jnp.dot(
                hidden, wbuf[slot, 2, :, columns], preferred_element_type=jnp.float32
            )
            rows[e, part, columns] = (result * scale).astype(jnp.bfloat16)

        @pl.when(t + WBUF < 2 * experts)
        def _():
            for copy in weight_copies(lax.rem(t + WBUF, experts), slot):
                copy.start()

    def run_experts(half, first, last):
        def step(t, carry):
            expert_step(t, half)
            return carry

        lax.fori_loop(half * experts + first, half * experts + last, step, 0)

    def combine(q):
        base = pl.multiple_of(q * pair_slots, pair_slots)

        def part(n, carry):
            columns = pl.ds(pl.multiple_of(n * CHUNK, CHUNK), CHUNK)
            block = rows[:, pl.ds(base, pair_slots), columns].reshape(
                experts * pair_slots, CHUNK
            )
            got = jnp.dot(pickt[q], block, preferred_element_type=jnp.float32)
            got = got.astype(jnp.bfloat16)
            done[2 * q + c_me, :, columns] = got[:tok]
            done[2 * q + 1 - c_me, :, columns] = got[tok:]
            return carry

        lax.fori_loop(0, width // CHUNK, part, 0)

    def r1_copy(q):
        return remote(
            done.at[2 * q + 1], core_buf.at[q], r1_send.at[q], r1_recv.at[q], e_me, f_cn
        )

    def r2_copy(j):
        return remote(
            done.at[4 * j + 2], x_buf.at[j], r2_send.at[j], r2_recv.at[j], e_me, f_xn
        )

    def r3_copy(j):
        return remote(
            done.at[4 * j], z_buf.at[lax.rem(e_me + 4 - group(j), 4) - 1], r3_send.at[j - 1], r3_recv.at[e_me], group(j), f_me,
        )

    def finish(j):
        r1_copy(2 * j).wait_recv()
        r2_copy(j).wait_recv()
        return (
            done[4 * j].astype(jnp.float32)
            + core_buf[2 * j].astype(jnp.float32)
            + x_buf[j].astype(jnp.float32)
        )

    def emit(j):
        combine(2 * j + 1)
        r1_copy(2 * j + 1).start()
        combine(2 * j)
        r1_copy(2 * j).start()

    def emit_across(j):
        r1_copy(2 * j + 1).wait_recv()
        done[4 * j + 2] = (
            done[4 * j + 2].astype(jnp.float32) + core_buf[2 * j + 1].astype(jnp.float32)
        ).astype(jnp.bfloat16)
        r2_copy(j).start()

    def emit_along(j):
        done[4 * j] = finish(j).astype(jnp.bfloat16)
        r3_copy(j).start()

    quarter = experts // 4
    take(0, 0)
    pass_across(0)
    pass_on(1)
    take(0, 1)
    take(1, 0)
    pass_across(1)
    pass_on(2)
    take(1, 1)
    run_experts(0, 0, quarter)
    pass_across(2)
    pass_on(3)
    run_experts(0, quarter, 3 * quarter)
    pass_across(3)
    run_experts(0, 3 * quarter, experts)
    emit(1)
    emit(0)
    emit_across(1)
    emit_across(0)
    for j in (2, 3):
        take(j, 0)
        take(j, 1)
    run_experts(1, 0, 3 * quarter)
    emit_along(1)
    run_experts(1, 3 * quarter, experts)
    emit(3)
    emit_across(3)
    emit(2)
    emit_across(2)
    emit_along(3)
    emit_along(2)
    total = finish(0)
    for k in (1, 2, 3):
        source = lax.rem(e_me + k, 4)
        remote(
            done.at[0], z_buf.at[k - 1], r3_send.at[0], r3_recv.at[source], source, f_me
        ).wait_recv()
        total = total + z_buf[k - 1].astype(jnp.float32)
    out_ref[...] = total.astype(jnp.bfloat16)
    for i in range(1, 16):
        meta_copy(i).wait_send()
    for j in range(4):
        relay(group(j), lambda copy: copy.wait_send())
        x_copy(j).wait_send()
        c_copy(j, 0).wait_send()
        c_copy(j, 1).wait_send()
    for q in range(8):
        r1_copy(q).wait_send()
    for j in range(4):
        r2_copy(j).wait_send()
    for j in (1, 2, 3):
        r3_copy(j).wait_send()


def on_device_fused(tokens, expert_ids, gate_values, w_gate, w_up, w_down):
    tok, width = tokens.shape
    experts, ff = w_down.shape[:2]
    packed = jnp.concatenate([expert_ids.T.astype(jnp.float32), gate_values.T], axis=0)
    bf16, f32 = jnp.bfloat16, jnp.float32
    dma = pltpu.SemaphoreType.DMA
    vmem = pl.BlockSpec(memory_space=pltpu.VMEM)
    hbm = pl.BlockSpec(memory_space=pl.ANY)
    slots = 16 * ECAP
    return pl.pallas_call(
        fused_kernel,
        out_shape=jax.ShapeDtypeStruct((tok, width), bf16),
        in_specs=[hbm, vmem, hbm, hbm, hbm],
        out_specs=vmem,
        scratch_shapes=[
            pltpu.VMEM((16, tok, width), bf16),
            pltpu.VMEM((16,) + packed.shape, f32),
            pltpu.VMEM((experts, slots, width), bf16),
            pltpu.VMEM((experts, slots // 2, 128), f32),
            pltpu.VMEM((experts * 2 * ECAP, 2 * tok), f32),
            pltpu.VMEM((8, 2 * tok, experts * 2 * ECAP), bf16),
            pltpu.VMEM((WBUF, 3, ff, width), bf16),
            pltpu.VMEM((8, tok, width), bf16),
            pltpu.VMEM((4, tok, width), bf16),
            pltpu.VMEM((3, tok, width), bf16),
            pltpu.VMEM((16, tok, width), bf16),
            dma((2,)), dma((WBUF, 3)), dma((15,)), dma((15,)),
            dma((4,)), dma((4,)), dma((4,)), dma((4,)), dma((4,)), dma((8,)), dma((8,)),
            dma((8,)), dma((8,)), dma((4,)), dma((4,)), dma((3,)), dma((4,)),
        ],
        compiler_params=pltpu.CompilerParams(
            collective_id=0, has_side_effects=True, vmem_limit_bytes=63 * 1024 * 1024
        ),
    )(tokens, packed, w_gate.swapaxes(1, 2), w_up.swapaxes(1, 2), w_down)


def on_device(tokens, expert_ids, gate_values, w_gate, w_up, w_down):
    row_count, model_width = tokens.shape
    top_count = expert_ids.shape[1]
    local_count = w_gate.shape[0]
    axes = ("ep", "fs")
    blocks = lax.axis_size("ep") * lax.axis_size("fs")
    packed = jnp.concatenate([expert_ids.astype(jnp.float32), gate_values], axis=1)
    all_tokens = lax.all_gather(tokens, axes, axis=0, tiled=False)
    all_packed = lax.all_gather(packed, axes, axis=0, tiled=False)
    ids = all_packed[:, :, :top_count].astype(jnp.int32)
    gates = all_packed[:, :, top_count:]
    mine = lax.axis_index("ep") * local_count + jnp.arange(local_count, dtype=jnp.int32)
    match = ids[:, :, :, None] == mine
    member = jnp.any(match, axis=2)
    weight = jnp.sum(jnp.where(match, gates[:, :, :, None], 0.0), axis=2)
    place = jnp.cumsum(member.astype(jnp.int32), axis=1) - 1
    place = jnp.where(member, place, -1)
    pick = place.transpose(0, 2, 1)[:, :, None, :] == jnp.arange(ECAP, dtype=jnp.int32)[:, None]
    slot_weight = jnp.sum(
        jnp.where(pick, weight.transpose(0, 2, 1)[:, :, None, :], 0.0), axis=3
    )
    pick = pick.astype(jnp.bfloat16)
    rows = jnp.einsum("best,btd->besd", pick, all_tokens)
    rows = rows.transpose(1, 0, 2, 3).reshape(local_count, blocks * ECAP, model_width)
    gate_part = jnp.einsum("erd,edf->erf", rows, w_gate, preferred_element_type=jnp.float32)
    up_part = jnp.einsum("erd,edf->erf", rows, w_up, preferred_element_type=jnp.float32)
    hidden = (jax.nn.silu(gate_part) * up_part).astype(jnp.bfloat16)
    results = jnp.einsum("erf,efd->erd", hidden, w_down, preferred_element_type=jnp.float32)
    results = results.reshape(local_count, blocks, ECAP, model_width)
    results = (results * slot_weight.transpose(1, 0, 2)[:, :, :, None]).astype(jnp.bfloat16)
    partial = jnp.einsum(
        "best,ebsd->btd", pick, results, preferred_element_type=jnp.float32
    ).astype(jnp.bfloat16)
    summed = lax.psum_scatter(
        partial.reshape(blocks * row_count, model_width), axes, scatter_dimension=0, tiled=True
    )
    return summed


def solution(mesh):
    placed = (
        P(("grp", "ep", "fs"), None),
        P(("grp", "ep", "fs"), None),
        P(("grp", "ep", "fs"), None),
        P("ep", None, "fs"),
        P("ep", None, "fs"),
        P("ep", "fs", None),
    )
    small = mesh.shape["ep"] == 4 and mesh.shape["fs"] == 4
    return jax.shard_map(
        on_device_fused if small else on_device,
        mesh=mesh,
        in_specs=placed,
        out_specs=P(("grp", "ep", "fs"), None),
        check_vma=False,
    )
```
